32 devices in a mesh: grp: 4 (over y, x), dev: 8 (over z, core).
Axes of the slice: x: 2, y: 2, z: 4, core: 2. Of those that a mesh axis runs over, the one named last changes fastest.
Arguments:
- particles: float32 [128, 5, 128], P(('grp', 'dev')), as said below
- entropy: float32 [128, 128], P(('grp', 'dev')), may hold values from 0.5 to 2
- lists: int32 [128, 64], P(('grp', 'dev')), may hold values from 0 to 127, as said below
- counts: int32 [128], P(('grp', 'dev')), may hold values from 16 to 64, as said below
Outputs:
- density: float32 [128, 128], P(('grp', 'dev'))
- accel: float32 [128, 3, 128], P(('grp', 'dev'))
The draws below stay inside these ranges and needn't reach their ends.
Inputs may be any that keep to these rules, and one draw needn't show every extreme that they name: lists[c, 0] = c; every id lies in the group of c or in one of the two groups next to it, counting groups of 32 cells around a loop. `counts`: each count is a multiple of 16. `particles`: coordinates in 0 to 1 within the group's slab, masses positive, smoothing lengths from 0.3 to 0.6.
All inputs are finite; a program needn't handle non-finite values.
Results may differ from the reference program's by a relative error of at most 0.0003.
Values sent between devices are 32-bit elements; how exact they have to be, the bound alone decides.
No kernel may reach another device: no remote copies, remote signals or barrier semaphores. Data moves between devices by JAX's collectives and lax.ppermute only.
A program may use at most 64 MiB of HBM per device.

```python
import math
import jax
import jax.numpy as jnp
from jax import lax

P_SIZE = 128
NB = 64
CG = 32
CELLS = 128
N_GRP = 4


def draw_particles(key, part):
    key_pos = jax.random.fold_in(key, 11)
    key_mass = jax.random.fold_in(key, 12)
    key_smooth = jax.random.fold_in(key, 13)
    coords = jax.random.uniform(key_pos, (CELLS, 3, P_SIZE), jnp.float32)
    mass_log = jax.random.uniform(key_mass, (CELLS, 1, P_SIZE), jnp.float32, jnp.log(0.0003), jnp.log(0.0015))
    smooth = jax.random.uniform(key_smooth, (CELLS, 1, P_SIZE), jnp.float32, 0.3, 0.6)
    return jnp.concatenate([coords, jnp.exp(mass_log), smooth], axis=1).astype(jnp.float32)


def draw_lists(key, part):
    key_side = jax.random.fold_in(key, 21)
    key_rest = jax.random.fold_in(key, 22)
    cell_ids = jnp.arange(CELLS, dtype=jnp.int32)
    group_of = cell_ids // CG
    pick = jax.random.randint(key_side, (CELLS, NB), 0, 10, dtype=jnp.int32)
    shift_by = jnp.where(pick == 0, -1, jnp.where(pick == 1, 1, 0)).astype(jnp.int32)
    target = (group_of[:, None] + shift_by + N_GRP) % N_GRP
    within = jax.random.randint(key_rest, (CELLS, NB), 0, CG, dtype=jnp.int32)
    chosen = target * CG + within
    return chosen.at[:, 0].set(cell_ids).astype(jnp.int32)


def draw_counts(key, part):
    key_len = jax.random.fold_in(key, 31)
    quarter = jax.random.randint(key_len, (CELLS,), 1, 5, dtype=jnp.int32)
    values = quarter * (NB // 4)
    return values.at[0].set(NB).astype(jnp.int32)


def shard_levels(key, dims, pieces, low, high):
    gain = 1.0
    for axis_at, parts in pieces:
        heights = jax.random.uniform(jax.random.fold_in(jax.random.fold_in(key, 6), axis_at), (parts,), jnp.float32, low / len(pieces), high / len(pieces))
        gain = gain * jnp.repeat(jnp.exp(heights), dims[axis_at] // parts).reshape((-1,) + (1,) * (len(dims) - 1 - axis_at))
    return gain


def setup_inputs(seed: int = 0) -> dict:
    key_list = jax.random.split(jax.random.key(seed), 5)
    particles = draw_particles(jax.random.fold_in(key_list[4], 71), 0)
    entropy = jnp.clip(jnp.exp(math.log(2.0) - 1.3862944 * jax.random.uniform(key_list[1], (CELLS, P_SIZE), jnp.float32) ** shard_levels(key_list[1], (CELLS, P_SIZE), ((0, 32),), -0.2, 0.2)), 0.5, 2.0)
    lists = draw_lists(jax.random.fold_in(key_list[4], 71), 0)
    counts = draw_counts(jax.random.fold_in(key_list[4], 71), 0)
    return dict(particles=particles, entropy=entropy, lists=lists, counts=counts)


norm_const = 21.0 / (16.0 * math.pi)

def pair_offsets(center, others, side):
    unit_first = jnp.array([1.0, 0.0, 0.0], dtype=jnp.float32)
    offset = center[None, :3, :, None] - others[:, :3, None, :]
    offset = offset - side[:, None, None, None] * unit_first[None, :, None, None]
    dist_sq = lax.optimization_barrier(jnp.sum(offset * offset, axis=1))
    return (offset, dist_sq)

def kernel_parts(dist_sq, smooth):
    ratio = jnp.sqrt(dist_sq) / smooth
    base_of = jnp.maximum(1.0 - 0.5 * ratio, 0.0)
    kernel = norm_const / smooth ** 3 * base_of ** 4 * (1.0 + 2.0 * ratio)
    slope = -5.0 * norm_const / smooth ** 5 * base_of ** 3
    return (kernel, slope)

def reference(particles, entropy, lists, counts):
    slot_ids = jnp.arange(NB, dtype=jnp.int32)

    def side_for(cell_id):
        ids = lists[cell_id]
        shift = (ids // CG - cell_id // CG + 1 + N_GRP) % N_GRP - 1
        return shift.astype(jnp.float32)

    def density_cell(cell_id):
        center = particles[cell_id]
        others = particles[lists[cell_id]]
        live = (slot_ids < counts[cell_id]).astype(jnp.float32)
        offset, dist_sq = pair_offsets(center, others, side_for(cell_id))
        kernel, slope = kernel_parts(dist_sq, center[4][None, :, None])
        return lax.optimization_barrier(jnp.sum(live[:, None, None] * others[:, 3][:, None, :] * kernel, axis=(0, 2)))
    cell_range = jnp.arange(CELLS, dtype=jnp.int32)
    density = lax.map(density_cell, cell_range)
    pressure = entropy * density ** (5.0 / 3.0)
    weight = pressure / (density * density)

    def force_cell(cell_id):
        center = particles[cell_id]
        others = particles[lists[cell_id]]
        live = (slot_ids < counts[cell_id]).astype(jnp.float32)
        offset, dist_sq = pair_offsets(center, others, side_for(cell_id))
        kernel_i, slope_i = kernel_parts(dist_sq, center[4][None, :, None])
        kernel_j, slope_j = kernel_parts(dist_sq, others[:, 4][:, None, :])
        factor = live[:, None, None] * others[:, 3][:, None, :] * (weight[cell_id][None, :, None] * slope_i + weight[lists[cell_id]][:, None, :] * slope_j)
        return -lax.optimization_barrier(jnp.sum(factor[:, None] * offset, axis=(0, 3)))
    accel = lax.map(force_cell, cell_range)
    return (density, accel)
```

```python
import functools
import math

import jax
import jax.numpy as jnp
from jax import lax
from jax.experimental import pallas as pl
from jax.experimental.pallas import tpu as pltpu
from jax.sharding import Mesh
from jax.sharding import PartitionSpec as P

NORM = 21.0 / (16.0 * math.pi)
TINY = 1e-30
ROWS = 8
UNROLL = 4


def split3(v):
    hi = v.astype(jnp.bfloat16).astype(jnp.float32)
    rest = v - hi
    mid = rest.astype(jnp.bfloat16).astype(jnp.float32)
    return hi, mid, rest - mid


def right_parts(v):
    hi, mid, low = split3(v)
    return jnp.concatenate([hi, mid, hi, low, hi, mid], axis=0).astype(jnp.bfloat16)


def left_parts(v):
    hi, mid, low = split3(v)
    stacked = jnp.concatenate([hi, hi, mid, hi, low, mid], axis=0)
    return jnp.transpose(stacked).astype(jnp.bfloat16)


def sum_parts(v):
    hi, mid, low = split3(v)
    return jnp.concatenate([hi, mid, low, jnp.zeros_like(low)], axis=0).astype(jnp.bfloat16)


def left_rows(v):
    row = lax.broadcasted_iota(jnp.int32, v.shape, 0)
    out = jnp.where(row < 3, -2.0 * v, jnp.where(row == 3, v[4:5], jnp.where(row == 4, 1.0, 0.0)))
    return out


def right_rows(v, shift):
    row = lax.broadcasted_iota(jnp.int32, v.shape, 0)
    moved = jnp.where(row == 0, shift, jnp.where(row == 4, shift * (2.0 * v[0:1] + shift), 0.0))
    return jnp.where(row < 5, v, 0.0) + moved


def table_index(cell_id, place, sizes):
    groups, depth, cores, own = sizes
    group_cells = depth * cores * own
    group_at, z_at, core_at = place[0], place[1], place[2]
    side = lax.rem(lax.div(cell_id, group_cells) - group_at + 1 + groups, groups)
    within = lax.rem(cell_id, group_cells)
    member = lax.div(within, own)
    z = lax.rem(lax.div(member, cores) - z_at + depth, depth)
    core = lax.rem(lax.rem(member, cores) - core_at + cores, cores)
    return ((side * cores + core) * depth + z) * own + lax.rem(within, own)


def table_cells(refs, sizes, fn):
    _, depth, cores, own = sizes
    per_ref = depth * own
    for at, ref in enumerate(refs):
        shift = float(at // cores - 1)

        def step(i, carry, ref=ref, at=at, shift=shift):
            fn(at * per_ref + i, ref[i], shift)
            return carry

        lax.fori_loop(0, per_ref, step, 0, unroll=4)


def density_kernel(sizes, place, lists, counts, own_ref, entropy, *rest):
    refs, (density, weight, table, nu_rows) = rest[:-4], rest[-4:]

    def fill(at, v, shift):
        nu = v[7:8]
        table[at] = right_parts((nu * nu) * right_rows(v, shift))
        nu_rows[at] = jnp.broadcast_to(nu, v.shape)

    table_cells(refs, sizes, fill)
    own = sizes[3]
    width = own_ref.shape[2]
    for cell in range(own):
        v = own_ref[cell]
        smooth = v[6:7]
        left = left_parts((4.0 / (smooth * smooth)) * left_rows(v))

        def step(k, total, cell=cell, left=left):
            for pair in range(UNROLL // 2):
                slot = k * UNROLL + 2 * pair
                at = [table_index(lists[cell, slot + e], place, sizes) for e in range(2)]
                right = jnp.concatenate([table[at[0]], table[at[1]]], axis=1)
                nu = jnp.concatenate([nu_rows[at[0]][:1], nu_rows[at[1]][:1]], axis=1)
                sq = jnp.maximum(jnp.dot(left, right, preferred_element_type=jnp.float32), TINY)
                base = jnp.maximum(4.0 * nu - sq * lax.rsqrt(sq), 0.0)
                base2 = base * base
                term = (base2 * base2) * (5.0 * nu - base)
                total = total + term[:, :width] + term[:, width:]
            return total

        total = lax.fori_loop(
            0, lax.div(counts[cell], UNROLL), step, jnp.zeros((width, width), jnp.float32)
        )
        summed = jnp.sum(jnp.transpose(total), axis=0, keepdims=True)
        dens = (NORM / 256.0) / (smooth * smooth * smooth) * summed
        density[cell : cell + 1] = dens
        weight[cell : cell + 1] = entropy[cell : cell + 1] * jnp.exp(jnp.log(dens) * (-1.0 / 3.0))


def pair_sums(left, cell, place, sizes, lists, counts, table, sums, width):
    def step(k, total):
        for pair in range(UNROLL // 2):
            slot = k * UNROLL + 2 * pair
            at = [table_index(lists[cell, slot + e], place, sizes) for e in range(2)]
            right = jnp.concatenate([table[at[0]], table[at[1]]], axis=1)
            rows = jnp.concatenate([sums[at[0]], sums[at[1]]], axis=1)
            sq = jnp.maximum(jnp.dot(left, right, preferred_element_type=jnp.float32), TINY)
            base = jnp.maximum(1.0 - sq * lax.rsqrt(sq), 0.0)
            cube = base * base * base
            hi = cube.astype(jnp.bfloat16)
            low = (cube - hi.astype(jnp.float32)).astype(jnp.bfloat16)
            total = total + lax.dot_general(
                jnp.concatenate([hi, low], axis=1),
                jnp.concatenate([rows, rows], axis=1),
                (((1,), (1,)), ((), ())),
                preferred_element_type=jnp.float32,
            )
        return total

    total = lax.fori_loop(
        0, lax.div(counts[cell], UNROLL), step, jnp.zeros((width, 4 * ROWS), jnp.float32)
    )
    total = jnp.transpose(total)
    return total[:ROWS] + total[ROWS : 2 * ROWS] + total[2 * ROWS : 3 * ROWS]


def own_kernel(sizes, place, lists, counts, own_ref, *rest):
    refs, (out, table, sums) = rest[:-3], rest[-3:]

    def fill(at, v, shift):
        rows = right_rows(v, shift)
        table[at] = right_parts(rows)
        sums[at] = sum_parts(v[5:6] * rows)

    table_cells(refs, sizes, fill)
    for cell in range(sizes[3]):
        v = own_ref[cell]
        smooth = v[6:7]
        left = left_parts((0.25 / (smooth * smooth)) * left_rows(v))
        out[cell] = pair_sums(
            left, cell, place, sizes, lists, counts, table, sums, own_ref.shape[2]
        )


def other_kernel(sizes, place, lists, counts, own_ref, weight_own, part, weight_all, *rest):
    refs, (out, table, sums) = rest[:-3], rest[-3:]
    groups, depth, cores, own = sizes
    per_ref = depth * own

    def fill(at, v, shift):
        ref_at, in_ref = lax.div(at, per_ref), lax.rem(at, per_ref)
        side, core = lax.div(ref_at, cores), lax.rem(ref_at, cores)
        group = lax.rem(place[0] + side - 1 + groups, groups)
        z = lax.rem(place[1] + lax.div(in_ref, own), depth)
        source = (group * depth + z) * cores + lax.rem(place[2] + core, cores)
        weight = weight_all[source, pl.ds(lax.rem(in_ref, own), 1), :]
        rows = right_rows(v, shift)
        inv = 1.0 / v[6:7]
        inv2 = inv * inv
        table[at] = right_parts((0.25 * inv2) * rows)
        sums[at] = sum_parts((v[5:6] * weight * (inv2 * inv2 * inv)) * rows)

    table_cells(refs, sizes, fill)
    for cell in range(own):
        v = own_ref[cell]
        left = left_parts(left_rows(v))
        other = pair_sums(
            left, cell, place, sizes, lists, counts, table, sums, own_ref.shape[2]
        )
        inv = 1.0 / v[6:7]
        inv2 = inv * inv
        total = (weight_own[cell : cell + 1] * (inv2 * inv2 * inv)) * part[cell] + other
        for k in range(3):
            out[k, cell : cell + 1, :] = (5.0 * NORM) * (
                v[k : k + 1] * total[3:4] - total[k : k + 1]
            )


def call(kernel, name, out_shape, scratch, place, lists, counts, arrays):
    smem = pl.BlockSpec(memory_space=pltpu.SMEM)
    vmem = pl.BlockSpec(memory_space=pltpu.VMEM)
    many = isinstance(out_shape, tuple)
    return pl.pallas_call(
        kernel,
        name=name,
        out_shape=out_shape,
        in_specs=[smem] * 3 + [vmem] * len(arrays),
        out_specs=(vmem,) * len(out_shape) if many else vmem,
        scratch_shapes=scratch,
        cost_estimate=pl.CostEstimate(
            flops=4_000_000_000, bytes_accessed=4_000_000, transcendentals=4_000_000
        ),
    )(place, lists, counts, *arrays)


def on_device(particles, entropy, lists, counts):
    own, _, width = particles.shape
    groups, depth, cores = (lax.axis_size(a) for a in ("grp", "z", "core"))
    sizes = (groups, depth, cores, own)
    place = jnp.stack([lax.axis_index(a) for a in ("grp", "z", "core")]).astype(jnp.int32)

    coords = particles[:, :3] - 0.5
    mass, smooth = particles[:, 3:4], particles[:, 4:5]
    rows = jnp.concatenate(
        [
            coords,
            jnp.ones_like(mass),
            jnp.sum(coords * coords, axis=1, keepdims=True),
            mass,
            smooth,
            jnp.exp(jnp.log(mass) * 0.2),
        ],
        axis=1,
    )

    def shifted(block, axis, by):
        count = lax.axis_size(axis)
        return lax.ppermute(block, axis, [(i, (i - by) % count) for i in range(count)])

    order = [1, depth - 1] + list(range(2, depth - 1))
    got = {0: rows}
    for by in dict.fromkeys(b % depth for b in order):
        if by:
            got[by] = shifted(rows, "z", by)
    column = jnp.concatenate([got[by] for by in range(depth)], axis=0)
    sides = [shifted(column, "grp", -1), column, shifted(column, "grp", 1)]
    refs = []
    for side in sides:
        refs.append(side)
        for by in range(1, cores):
            refs.append(shifted(side, "core", by))

    cells = 3 * cores * depth * own
    shape = jax.ShapeDtypeStruct
    table = pltpu.VMEM((cells, 6 * ROWS, width), jnp.bfloat16)
    sums = pltpu.VMEM((cells, 4 * ROWS, width), jnp.bfloat16)
    density, weight = call(
        functools.partial(density_kernel, sizes),
        "density",
        (shape((own, width), jnp.float32), shape((own, width), jnp.float32)),
        [table, pltpu.VMEM((cells, ROWS, width), jnp.float32)],
        place,
        lists,
        counts,
        [rows, entropy, *refs],
    )
    everyone = groups * depth * cores
    weight_all = lax.all_to_all(
        jnp.broadcast_to(weight[None], (everyone, own, width)),
        ("grp", "z", "core"),
        0,
        0,
        tiled=True,
    )
    part = call(
        functools.partial(own_kernel, sizes),
        "own",
        shape((own, ROWS, width), jnp.float32),
        [table, sums],
        place,
        lists,
        counts,
        [rows, *refs],
    )
    accel = call(
        functools.partial(other_kernel, sizes),
        "other",
        shape((3, own, width), jnp.float32),
        [table, sums],
        place,
        lists,
        counts,
        [rows, weight, part, weight_all, *refs],
    )
    return density, jnp.transpose(accel, (1, 0, 2))


def solution(mesh):
    groups, members = mesh.devices.shape
    cores = 2 if members % 2 == 0 else 1
    split = Mesh(mesh.devices.reshape(groups, members // cores, cores), ("grp", "z", "core"))
    cells = ("grp", "z", "core")
    return jax.shard_map(
        on_device,
        mesh=split,
        in_specs=(P(cells, None, None), P(cells, None), P(cells, None), P(cells)),
        out_specs=(P(cells, None), P(cells, None, None)),
        check_vma=False,
    )
```

```python
import functools
import math

import jax
import jax.numpy as jnp
from jax import lax
from jax.experimental import pallas as pl
from jax.experimental.pallas import tpu as pltpu
from jax.sharding import Mesh
from jax.sharding import PartitionSpec as P

NORM = 21.0 / (16.0 * math.pi)
TINY = 1e-30
ROWS = 8
BATCH = 16
CHUNK = 16
VMEM_LIMIT = 24 * 1024 * 1024


def split3(v):
    hi = v.astype(jnp.bfloat16).astype(jnp.float32)
    rest = v - hi
    mid = rest.astype(jnp.bfloat16).astype(jnp.float32)
    return hi, mid, rest - mid


def right_parts(v):
    hi, mid, low = split3(v)
    return jnp.concatenate([hi, mid, hi, low, hi, mid], axis=0)


def left_parts(v):
    hi, mid, low = split3(v)
    return jnp.concatenate([hi, hi, mid, hi, low, mid], axis=0)


def sum_parts(v):
    hi, mid, low = split3(v)
    return jnp.concatenate([hi, mid, low, jnp.zeros_like(low)], axis=0).astype(jnp.bfloat16)


def left_rows(v):
    row = lax.broadcasted_iota(jnp.int32, v.shape, 0)
    return jnp.where(row < 3, -2.0 * v, jnp.where(row == 3, v[4:5], jnp.where(row == 4, 1.0, 0.0)))


def right_rows(v, shift):
    row = lax.broadcasted_iota(jnp.int32, v.shape, 0)
    rows = jnp.where(row < 5, v, 0.0)
    if shift:
        rows = rows + jnp.where(
            row == 0, shift, jnp.where(row == 4, shift * (2.0 * v[0:1] + shift), 0.0)
        )
    return rows


def table_cells(refs, sizes, fn):
    _, depth, cores, own = sizes
    per_ref = depth * own
    for at, ref in enumerate(refs):
        shift = float(at // cores - 1)

        def step(i, carry, ref=ref, at=at, shift=shift):
            fn(at * per_ref + i, ref[i], shift)
            return carry

        lax.fori_loop(0, per_ref, step, 0, unroll=4)


def list_batches(own, counts, cell_of, slot_of):
    made = jnp.int32(0)
    for cell in range(own):

        def step(k, made, cell=cell):
            cell_of[made] = cell
            slot_of[made] = k * BATCH
            return made + 1

        made = lax.fori_loop(0, lax.div(counts[cell], BATCH), step, made)
    return made


def density_kernel(sizes, index, counts, own_ref, entropy, *rest):
    refs, (density, weight, table, nu_rows, left, total, ahead, cell_of, slot_of) = (
        rest[:-9],
        rest[-9:],
    )
    own = sizes[3]
    width = own_ref.shape[2]

    def fill(at, v, shift):
        nu = v[7:8]
        table[at] = right_parts((nu * nu) * right_rows(v, shift)).astype(jnp.bfloat16)
        nu_rows[at] = jnp.broadcast_to(nu, v.shape)

    table_cells(refs, sizes, fill)
    for cell in range(own):
        v = own_ref[cell]
        parts = left_parts((4.0 / (v[6:7] * v[6:7])) * left_rows(v))
        left[cell] = jnp.transpose(parts).astype(jnp.bfloat16)
    total[...] = jnp.zeros_like(total)
    batches = list_batches(own, counts, cell_of, slot_of)

    def slots(batch, pair):
        cell, slot = cell_of[batch], slot_of[batch] + 2 * pair
        return index[cell, slot], index[cell, slot + 1]

    def squares(batch, pair):
        first, second = slots(batch, pair)
        right = jnp.concatenate([table[first], table[second]], axis=1)
        return jnp.dot(left[cell_of[batch]], right, preferred_element_type=jnp.float32)

    for pair in range(BATCH // 2):
        ahead[pair] = squares(0, pair)

    def step(batch, carry):
        later = jnp.minimum(batch + 1, batches - 1)
        sums = [None] * (width // CHUNK)
        for pair in range(BATCH // 2):
            first, second = slots(batch, pair)
            nu = jnp.concatenate([nu_rows[first][:1], nu_rows[second][:1]], axis=1)
            nu4 = jnp.broadcast_to(4.0 * nu, (CHUNK, 2 * width))
            nu5 = jnp.broadcast_to(5.0 * nu, (CHUNK, 2 * width))
            for r in range(width // CHUNK):
                sq = jnp.maximum(ahead[pair, r * CHUNK : (r + 1) * CHUNK], TINY)
                base = jnp.maximum(nu4 - sq * lax.rsqrt(sq), 0.0)
                base2 = base * base
                term = (base2 * base2) * (nu5 - base)
                term = term[:, :width] + term[:, width:]
                sums[r] = term if sums[r] is None else sums[r] + term
        for pair in range(BATCH // 2):
            ahead[pair] = squares(later, pair)
        cell = cell_of[batch]
        for r in range(width // CHUNK):
            total[cell, r * CHUNK : (r + 1) * CHUNK] += sums[r]
        return carry

    lax.fori_loop(0, batches, step, 0)
    smooth = jnp.concatenate([own_ref[cell][6:7] for cell in range(own)], axis=0)
    summed = jnp.concatenate(
        [jnp.sum(jnp.transpose(total[cell]), axis=0, keepdims=True) for cell in range(own)], axis=0
    )
    dens = (NORM / 256.0) / (smooth * smooth * smooth) * summed
    density[...] = dens
    value = entropy[...] * jnp.exp(jnp.log(dens) * (-1.0 / 3.0))
    for copy in range(weight.shape[0]):
        weight[copy] = value


def pair_sums(sizes, index, counts, left, table, rows, total, ahead, cell_of, slot_of):
    own = sizes[3]
    width = table.shape[2]
    total[...] = jnp.zeros_like(total)
    batches = list_batches(own, counts, cell_of, slot_of)

    def slots(batch, pair):
        cell, slot = cell_of[batch], slot_of[batch] + 2 * pair
        return index[cell, slot], index[cell, slot + 1]

    def squares(batch, pair):
        first, second = slots(batch, pair)
        others = jnp.transpose(jnp.concatenate([table[first], table[second]], axis=0))
        return jnp.dot(others, left[cell_of[batch]], preferred_element_type=jnp.float32)

    for pair in range(BATCH // 2):
        ahead[pair] = squares(0, pair)

    def step(batch, carry):
        later = jnp.minimum(batch + 1, batches - 1)
        added = None
        for pair in range(BATCH // 2):
            highs, lows = [], []
            for r in range(width // CHUNK):
                sq = jnp.maximum(ahead[pair, r * CHUNK : (r + 1) * CHUNK], TINY)
                base = jnp.maximum(1.0 - sq * lax.rsqrt(sq), 0.0)
                cube = base * base * base
                high = cube.astype(jnp.bfloat16)
                highs.append(high)
                lows.append((cube - high.astype(jnp.float32)).astype(jnp.bfloat16))
            high = jnp.concatenate(highs, axis=0)
            low = jnp.concatenate(lows, axis=0)
            cubes = jnp.concatenate(
                [
                    jnp.concatenate([high[:, :width], high[:, width:]], axis=0),
                    jnp.concatenate([low[:, :width], low[:, width:]], axis=0),
                ],
                axis=1,
            )
            first, second = slots(batch, pair)
            both = jnp.concatenate([rows[first], rows[second]], axis=1)
            part = jnp.dot(both, cubes, preferred_element_type=jnp.float32)
            added = part if added is None else added + part
        for pair in range(BATCH // 2):
            ahead[pair] = squares(later, pair)
        total[cell_of[batch]] += added
        return carry

    lax.fori_loop(0, batches, step, 0)


def folded(total, width):
    both = total[:, :width] + total[:, width:]
    return both[:ROWS] + both[ROWS : 2 * ROWS] + both[2 * ROWS : 3 * ROWS]


def padded_parts(parts):
    pad = jnp.zeros((8 * ROWS - parts.shape[0], parts.shape[1]), parts.dtype)
    return jnp.concatenate([parts, pad], axis=0).astype(jnp.bfloat16)


def block_diagonal(parts):
    pad = jnp.zeros((8 * ROWS - parts.shape[0], parts.shape[1]), parts.dtype)
    whole = jnp.concatenate([parts, pad], axis=0)
    empty = jnp.zeros_like(whole)
    return jnp.concatenate(
        [
            jnp.concatenate([whole, empty], axis=1),
            jnp.concatenate([empty, whole], axis=1),
        ],
        axis=0,
    ).astype(jnp.bfloat16)


def own_kernel(sizes, index, counts, own_ref, *rest):
    refs, (out, left, table, rows, total, ahead, cell_of, slot_of) = rest[:-8], rest[-8:]

    def fill(at, v, shift):
        placed = right_rows(v, shift)
        table[at] = padded_parts(right_parts(placed))
        rows[at] = sum_parts(v[5:6] * placed)

    table_cells(refs, sizes, fill)
    for cell in range(sizes[3]):
        v = own_ref[cell]
        left[cell] = block_diagonal(left_parts((0.25 / (v[6:7] * v[6:7])) * left_rows(v)))
    pair_sums(sizes, index, counts, left, table, rows, total, ahead, cell_of, slot_of)
    for cell in range(sizes[3]):
        out[cell] = folded(total[cell], own_ref.shape[2])


def other_kernel(sizes, index, counts, place, own_ref, weight_own, part, weight_all, *rest):
    refs, (out, left, table, rows, total, ahead, cell_of, slot_of) = rest[:-8], rest[-8:]
    groups, depth, cores, own = sizes
    per_ref = depth * own

    def fill(at, v, shift):
        ref_at, in_ref = lax.div(at, per_ref), lax.rem(at, per_ref)
        side, core = lax.div(ref_at, cores), lax.rem(ref_at, cores)
        group = lax.rem(place[0] + side - 1 + groups, groups)
        z = lax.rem(place[1] + lax.div(in_ref, own), depth)
        source = (group * depth + z) * cores + lax.rem(place[2] + core, cores)
        weight = weight_all[source, pl.ds(lax.rem(in_ref, own), 1), :]
        placed = right_rows(v, shift)
        inv = 1.0 / v[6:7]
        inv2 = inv * inv
        table[at] = padded_parts(right_parts((0.25 * inv2) * placed))
        rows[at] = sum_parts((v[5:6] * weight * (inv2 * inv2 * inv)) * placed)

    table_cells(refs, sizes, fill)
    for cell in range(own):
        left[cell] = block_diagonal(left_parts(left_rows(own_ref[cell])))
    pair_sums(sizes, index, counts, left, table, rows, total, ahead, cell_of, slot_of)
    for cell in range(own):
        v = own_ref[cell]
        inv = 1.0 / v[6:7]
        inv2 = inv * inv
        scale = weight_own[0, cell : cell + 1] * (inv2 * inv2 * inv)
        both = scale * part[cell] + folded(total[cell], own_ref.shape[2])
        for k in range(3):
            out[k, cell : cell + 1, :] = (5.0 * NORM) * (
                v[k : k + 1] * both[3:4] - both[k : k + 1]
            )


def call(kernel, name, out_shape, scratch, scalars, arrays):
    smem = pl.BlockSpec(memory_space=pltpu.SMEM)
    vmem = pl.BlockSpec(memory_space=pltpu.VMEM)
    many = isinstance(out_shape, tuple)
    return pl.pallas_call(
        kernel,
        name=name,
        out_shape=out_shape,
        in_specs=[smem] * len(scalars) + [vmem] * len(arrays),
        out_specs=(vmem,) * len(out_shape) if many else vmem,
        scratch_shapes=scratch,
        compiler_params=pltpu.CompilerParams(vmem_limit_bytes=VMEM_LIMIT),
        cost_estimate=pl.CostEstimate(
            flops=4_000_000_000, bytes_accessed=4_000_000, transcendentals=4_000_000
        ),
    )(*scalars, *arrays)


def on_device(particles, entropy, lists, counts):
    own, _, width = particles.shape
    groups, depth, cores = (lax.axis_size(a) for a in ("grp", "z", "core"))
    sizes = (groups, depth, cores, own)
    place = jnp.stack([lax.axis_index(a) for a in ("grp", "z", "core")]).astype(jnp.int32)

    coords = particles[:, :3] - 0.5
    mass, smooth = particles[:, 3:4], particles[:, 4:5]
    rows = jnp.concatenate(
        [
            coords,
            jnp.ones_like(mass),
            jnp.sum(coords * coords, axis=1, keepdims=True),
            mass,
            smooth,
            jnp.exp(jnp.log(mass) * 0.2),
        ],
        axis=1,
    )

    def shifted(block, axis, by):
        count = lax.axis_size(axis)
        return lax.ppermute(block, axis, [(i, (i - by) % count) for i in range(count)])

    order = [1, depth - 1] + list(range(2, depth - 1))
    got = {0: rows}
    for by in dict.fromkeys(b % depth for b in order):
        if by:
            got[by] = shifted(rows, "z", by)
    column = jnp.concatenate([got[by] for by in range(depth)], axis=0)
    sides = [shifted(column, "grp", -1), column, shifted(column, "grp", 1)]
    refs = []
    for side in sides:
        refs.append(side)
        for by in range(1, cores):
            refs.append(shifted(side, "core", by))

    def table_index(cell_id):
        side = (cell_id // (depth * cores * own) - lax.axis_index("grp") + 1 + groups) % groups
        member = cell_id // own
        z = (member // cores - lax.axis_index("z") + depth) % depth
        core = (member - lax.axis_index("core") + cores) % cores
        return ((side * cores + core) * depth + z) * own + cell_id % own

    index = table_index(lists)
    cells = 3 * cores * depth * own
    shape = jax.ShapeDtypeStruct
    f32, bf16 = jnp.float32, jnp.bfloat16
    most = own * (lists.shape[1] // BATCH)
    order = [pltpu.SMEM((most,), jnp.int32), pltpu.SMEM((most,), jnp.int32)]
    ahead = pltpu.VMEM((BATCH // 2, width, 2 * width), f32)
    everyone = groups * depth * cores
    density, weight = call(
        functools.partial(density_kernel, sizes),
        "density",
        (shape((own, width), f32), shape((everyone, own, width), f32)),
        [
            pltpu.VMEM((cells, 6 * ROWS, width), bf16),
            pltpu.VMEM((cells, ROWS, width), f32),
            pltpu.VMEM((own, width, 6 * ROWS), bf16),
            pltpu.VMEM((own, width, width), f32),
            ahead,
            *order,
        ],
        [index, counts],
        [rows, entropy, *refs],
    )
    weight_all = lax.all_to_all(weight, ("grp", "z", "core"), 0, 0, tiled=True)
    scratch = [
        pltpu.VMEM((own, 16 * ROWS, 2 * width), bf16),
        pltpu.VMEM((cells, 8 * ROWS, width), bf16),
        pltpu.VMEM((cells, 4 * ROWS, width), bf16),
        pltpu.VMEM((own, 4 * ROWS, 2 * width), f32),
        ahead,
        *order,
    ]
    part = call(
        functools.partial(own_kernel, sizes),
        "own",
        shape((own, ROWS, width), f32),
        scratch,
        [index, counts],
        [rows, *refs],
    )
    accel = call(
        functools.partial(other_kernel, sizes),
        "other",
        shape((3, own, width), f32),
        scratch,
        [index, counts, place],
        [rows, weight, part, weight_all, *refs],
    )
    return density, jnp.transpose(accel, (1, 0, 2))


def solution(mesh):
    groups, members = mesh.devices.shape
    cores = 2 if members % 2 == 0 else 1
    split = Mesh(mesh.devices.reshape(groups, members // cores, cores), ("grp", "z", "core"))
    cells = ("grp", "z", "core")
    return jax.shard_map(
        on_device,
        mesh=split,
        in_specs=(P(cells, None, None), P(cells, None), P(cells, None), P(cells)),
        out_specs=(P(cells, None), P(cells, None, None)),
        check_vma=False,
    )
```

```python
import functools
import math

import jax
import jax.numpy as jnp
from jax import lax
from jax.experimental import pallas as pl
from jax.experimental.pallas import tpu as pltpu
from jax.sharding import Mesh
from jax.sharding import PartitionSpec as P


NORM = 21.0 / (16.0 * math.pi)
TINY = 1e-30
ROWS = 8
BATCH = 16
CHUNK = 16
VMEM_LIMIT = 24 * 1024 * 1024


def split3(v):
    hi = v.astype(jnp.bfloat16).astype(jnp.float32)
    rest = v - hi
    mid = rest.astype(jnp.bfloat16).astype(jnp.float32)
    return hi, mid, rest - mid


def right_parts(v):
    hi, mid, low = split3(v)
    return jnp.concatenate([hi, mid, hi, low, hi, mid], axis=0)


def left_parts(v):
    hi, mid, low = split3(v)
    return jnp.concatenate([hi, hi, mid, hi, low, mid], axis=0)


def sum_parts(v):
    hi, mid, low = split3(v)
    return jnp.concatenate([hi, mid, low, jnp.zeros_like(low)], axis=0).astype(jnp.bfloat16)


def left_rows(v):
    row = lax.broadcasted_iota(jnp.int32, v.shape, 0)
    return jnp.where(row < 3, -2.0 * v, jnp.where(row == 3, v[4:5], jnp.where(row == 4, 1.0, 0.0)))


def right_rows(v, shift):
    row = lax.broadcasted_iota(jnp.int32, v.shape, 0)
    rows = jnp.where(row < 5, v, 0.0)
    if shift:
        rows = rows + jnp.where(
            row == 0, shift, jnp.where(row == 4, shift * (2.0 * v[0:1] + shift), 0.0)
        )
    return rows


def table_cells(refs, sizes, fn):
    _, depth, cores, own = sizes
    per_ref = depth * own
    for at, ref in enumerate(refs):
        shift = float(at // cores - 1)

        def step(i, carry, ref=ref, at=at, shift=shift):
            fn(at * per_ref + i, ref[i], shift)
            return carry

        lax.fori_loop(0, per_ref, step, 0, unroll=4)


def list_batches(own, counts, cell_of, slot_of):
    made = jnp.int32(0)
    for cell in range(own):

        def step(k, made, cell=cell):
            cell_of[made] = cell
            slot_of[made] = k * BATCH
            return made + 1

        made = lax.fori_loop(0, lax.div(counts[cell], BATCH), step, made)
    return made


def rows_kernel(particles, rows):
    x, y, z, mass, smooth = (particles[k] for k in range(5))
    x, y, z = x - 0.5, y - 0.5, z - 0.5
    made = (x, y, z, jnp.ones_like(x), x * x + y * y + z * z, mass, 1.0 / smooth, jnp.exp(jnp.log(mass) * 0.2))
    for cell in range(particles.shape[1]):
        rows[cell] = jnp.concatenate([m[cell : cell + 1] for m in made], axis=0)


def density_kernel(sizes, index, counts, own_ref, entropy, *rest):
    refs, (density, weight, table, nu_rows, left, total, ahead, cell_of, slot_of) = (
        rest[:-9],
        rest[-9:],
    )
    own = sizes[3]
    width = own_ref.shape[2]

    def fill(at, v, shift):
        nu = v[7:8]
        table[at] = right_parts((nu * nu) * right_rows(v, shift)).astype(jnp.bfloat16)
        nu_rows[at] = jnp.broadcast_to(nu, v.shape)

    table_cells(refs, sizes, fill)
    for cell in range(own):
        v = own_ref[cell]
        parts = left_parts((4.0 * (v[6:7] * v[6:7])) * left_rows(v))
        left[cell] = jnp.transpose(parts).astype(jnp.bfloat16)
    total[...] = jnp.zeros_like(total)
    batches = list_batches(own, counts, cell_of, slot_of)

    def slots(batch, pair):
        cell, slot = cell_of[batch], slot_of[batch] + 2 * pair
        return index[cell, slot], index[cell, slot + 1]

    def squares(batch, pair):
        first, second = slots(batch, pair)
        right = jnp.concatenate([table[first], table[second]], axis=1)
        return jnp.dot(left[cell_of[batch]], right, preferred_element_type=jnp.float32)

    for pair in range(BATCH // 2):
        ahead[pair] = squares(0, pair)

    def step(batch, carry):
        later = jnp.minimum(batch + 1, batches - 1)
        sums = [None] * (width // CHUNK)
        for pair in range(BATCH // 2):
            first, second = slots(batch, pair)
            nu = jnp.concatenate([nu_rows[first][:1], nu_rows[second][:1]], axis=1)
            nu4 = jnp.broadcast_to(4.0 * nu, (CHUNK, 2 * width))
            nu5 = jnp.broadcast_to(5.0 * nu, (CHUNK, 2 * width))
            for r in range(width // CHUNK):
                sq = jnp.maximum(ahead[pair, r * CHUNK : (r + 1) * CHUNK], TINY)
                base = jnp.maximum(nu4 - sq * lax.rsqrt(sq), 0.0)
                base2 = base * base
                term = (base2 * base2) * (nu5 - base)
                term = term[:, :width] + term[:, width:]
                sums[r] = term if sums[r] is None else sums[r] + term
        for pair in range(BATCH // 2):
            ahead[pair] = squares(later, pair)
        cell = cell_of[batch]
        for r in range(width // CHUNK):
            total[cell, r * CHUNK : (r + 1) * CHUNK] += sums[r]
        return carry

    lax.fori_loop(0, batches, step, 0)
    inv = jnp.concatenate([own_ref[cell][6:7] for cell in range(own)], axis=0)
    summed = jnp.concatenate(
        [jnp.sum(jnp.transpose(total[cell]), axis=0, keepdims=True) for cell in range(own)], axis=0
    )
    dens = (NORM / 256.0) * (inv * inv * inv) * summed
    density[...] = dens
    value = entropy[...] * jnp.exp(jnp.log(dens) * (-1.0 / 3.0))
    for copy in range(weight.shape[0]):
        weight[copy] = value


def pair_sums(sizes, index, counts, left, table, rows, total, ahead, cell_of, slot_of):
    own = sizes[3]
    width = table.shape[2]
    total[...] = jnp.zeros_like(total)
    batches = list_batches(own, counts, cell_of, slot_of)

    def slots(batch, pair):
        cell, slot = cell_of[batch], slot_of[batch] + 2 * pair
        return index[cell, slot], index[cell, slot + 1]

    def squares(batch, pair):
        first, second = slots(batch, pair)
        others = jnp.transpose(jnp.concatenate([table[first], table[second]], axis=0))
        return jnp.dot(others, left[cell_of[batch]], preferred_element_type=jnp.float32)

    for pair in range(BATCH // 2):
        ahead[pair] = squares(0, pair)

    def step(batch, carry):
        later = jnp.minimum(batch + 1, batches - 1)
        added = None
        for pair in range(BATCH // 2):
            highs, lows = [], []
            for r in range(width // CHUNK):
                sq = jnp.maximum(ahead[pair, r * CHUNK : (r + 1) * CHUNK], TINY)
                base = jnp.maximum(1.0 - sq * lax.rsqrt(sq), 0.0)
                cube = base * base * base
                high = cube.astype(jnp.bfloat16)
                highs.append(high)
                lows.append((cube - high.astype(jnp.float32)).astype(jnp.bfloat16))
            high = jnp.concatenate(highs, axis=0)
            low = jnp.concatenate(lows, axis=0)
            cubes = jnp.concatenate(
                [
                    jnp.concatenate([high[:, :width], high[:, width:]], axis=0),
                    jnp.concatenate([low[:, :width], low[:, width:]], axis=0),
                ],
                axis=1,
            )
            first, second = slots(batch, pair)
            both = jnp.concatenate([rows[first], rows[second]], axis=1)
            part = jnp.dot(both, cubes, preferred_element_type=jnp.float32)
            added = part if added is None else added + part
        for pair in range(BATCH // 2):
            ahead[pair] = squares(later, pair)
        total[cell_of[batch]] += added
        return carry

    lax.fori_loop(0, batches, step, 0)


def folded(total, width):
    both = total[:, :width] + total[:, width:]
    return both[:ROWS] + both[ROWS : 2 * ROWS] + both[2 * ROWS : 3 * ROWS]


def padded_parts(parts):
    pad = jnp.zeros((8 * ROWS - parts.shape[0], parts.shape[1]), parts.dtype)
    return jnp.concatenate([parts, pad], axis=0).astype(jnp.bfloat16)


def block_diagonal(parts):
    pad = jnp.zeros((8 * ROWS - parts.shape[0], parts.shape[1]), parts.dtype)
    whole = jnp.concatenate([parts, pad], axis=0)
    empty = jnp.zeros_like(whole)
    return jnp.concatenate(
        [
            jnp.concatenate([whole, empty], axis=1),
            jnp.concatenate([empty, whole], axis=1),
        ],
        axis=0,
    ).astype(jnp.bfloat16)


def own_kernel(sizes, index, counts, own_ref, *rest):
    refs, (out, other_table, other_rows, left, table, rows, total, ahead, cell_of, slot_of) = (
        rest[:-10],
        rest[-10:],
    )

    def fill(at, v, shift):
        placed = right_rows(v, shift)
        inv2 = v[6:7] * v[6:7]
        table[at] = padded_parts(right_parts(placed))
        rows[at] = sum_parts(v[5:6] * placed)
        other_table[at] = padded_parts(right_parts((0.25 * inv2) * placed))
        other_rows[at] = (v[5:6] * (inv2 * inv2 * v[6:7])) * placed

    table_cells(refs, sizes, fill)
    for cell in range(sizes[3]):
        v = own_ref[cell]
        left[cell] = block_diagonal(left_parts((0.25 * (v[6:7] * v[6:7])) * left_rows(v)))
    pair_sums(sizes, index, counts, left, table, rows, total, ahead, cell_of, slot_of)
    for cell in range(sizes[3]):
        out[cell] = folded(total[cell], own_ref.shape[2])


def other_kernel(
    sizes,
    index,
    counts,
    place,
    own_ref,
    weight_own,
    part,
    weight_all,
    table,
    other_rows,
    out,
    left,
    rows,
    total,
    ahead,
    cell_of,
    slot_of,
):
    groups, depth, cores, own = sizes
    for block in range(3 * cores):
        side, core = block // cores, block % cores
        group = lax.rem(place[0] + side - 1 + groups, groups)

        def fill(step, carry, block=block, core=core, group=group):
            z = lax.rem(place[1] + step, depth)
            source = (group * depth + z) * cores + lax.rem(place[2] + core, cores)
            for cell in range(own):
                at = (block * depth + step) * own + cell
                rows[at] = sum_parts(weight_all[source, cell : cell + 1] * other_rows[at])
            return carry

        lax.fori_loop(0, depth, fill, 0, unroll=2)
    for cell in range(own):
        left[cell] = block_diagonal(left_parts(left_rows(own_ref[cell])))
    pair_sums(sizes, index, counts, left, table, rows, total, ahead, cell_of, slot_of)
    for cell in range(own):
        v = own_ref[cell]
        inv2 = v[6:7] * v[6:7]
        scale = weight_own[0, cell : cell + 1] * (inv2 * inv2 * v[6:7])
        both = scale * part[cell] + folded(total[cell], own_ref.shape[2])
        for k in range(3):
            out[k, cell : cell + 1, :] = (5.0 * NORM) * (
                v[k : k + 1] * both[3:4] - both[k : k + 1]
            )


def call(kernel, out_shape, scratch, scalars, arrays):
    smem = pl.BlockSpec(memory_space=pltpu.SMEM)
    vmem = pl.BlockSpec(memory_space=pltpu.VMEM)
    many = isinstance(out_shape, tuple)
    return pl.pallas_call(
        kernel,
        out_shape=out_shape,
        in_specs=[smem] * len(scalars) + [vmem] * len(arrays),
        out_specs=(vmem,) * len(out_shape) if many else vmem,
        scratch_shapes=scratch,
        compiler_params=pltpu.CompilerParams(vmem_limit_bytes=VMEM_LIMIT),
        cost_estimate=pl.CostEstimate(
            flops=4_000_000_000, bytes_accessed=4_000_000, transcendentals=4_000_000
        ),
    )(*scalars, *arrays)


def on_device(particles, entropy, lists, counts):
    own, _, width = particles.shape
    groups, depth, cores = (lax.axis_size(a) for a in ("grp", "z", "core"))
    sizes = (groups, depth, cores, own)
    place = jnp.stack([lax.axis_index(a) for a in ("grp", "z", "core")]).astype(jnp.int32)

    rows = call(
        rows_kernel,
        jax.ShapeDtypeStruct((own, ROWS, width), jnp.float32),
        [],
        [],
        [jnp.transpose(particles, (1, 0, 2))],
    )

    def shifted(block, axis, by):
        count = lax.axis_size(axis)
        return lax.ppermute(block, axis, [(i, (i - by) % count) for i in range(count)])

    got = {0: rows}
    for by in range(1, depth):
        got[by] = shifted(rows, "z", by)
    column = jnp.concatenate([got[by] for by in range(depth)], axis=0)
    sides = [shifted(column, "grp", -1), column, shifted(column, "grp", 1)]
    refs = []
    for side in sides:
        refs.append(side)
        for by in range(1, cores):
            refs.append(shifted(side, "core", by))

    def table_index(cell_id):
        side = (cell_id // (depth * cores * own) - lax.axis_index("grp") + 1 + groups) % groups
        member = cell_id // own
        z = (member // cores - lax.axis_index("z") + depth) % depth
        core = (member - lax.axis_index("core") + cores) % cores
        return ((side * cores + core) * depth + z) * own + cell_id % own

    index = table_index(lists)
    cells = 3 * cores * depth * own
    shape = jax.ShapeDtypeStruct
    f32, bf16 = jnp.float32, jnp.bfloat16
    most = own * (lists.shape[1] // BATCH)
    order = [pltpu.SMEM((most,), jnp.int32), pltpu.SMEM((most,), jnp.int32)]
    ahead = pltpu.VMEM((BATCH // 2, width, 2 * width), f32)
    everyone = groups * depth * cores
    density, weight = call(
        functools.partial(density_kernel, sizes),
        (shape((own, width), f32), shape((everyone, own, width), f32)),
        [
            pltpu.VMEM((cells, 6 * ROWS, width), bf16),
            pltpu.VMEM((cells, ROWS, width), f32),
            pltpu.VMEM((own, width, 6 * ROWS), bf16),
            pltpu.VMEM((own, width, width), f32),
            ahead,
            *order,
        ],
        [index, counts],
        [rows, entropy, *refs],
    )
    weight_all = lax.all_to_all(weight, ("grp", "z", "core"), 0, 0, tiled=True)
    left = pltpu.VMEM((own, 16 * ROWS, 2 * width), bf16)
    table = (cells, 8 * ROWS, width)
    sums = pltpu.VMEM((cells, 4 * ROWS, width), bf16)
    total = pltpu.VMEM((own, 4 * ROWS, 2 * width), f32)
    part, other_table, other_rows = call(
        functools.partial(own_kernel, sizes),
        (shape((own, ROWS, width), f32), shape(table, bf16), shape((cells, ROWS, width), f32)),
        [left, pltpu.VMEM(table, bf16), sums, total, ahead, *order],
        [index, counts],
        [rows, *refs],
    )
    accel = call(
        functools.partial(other_kernel, sizes),
        shape((3, own, width), f32),
        [left, sums, total, ahead, *order],
        [index, counts, place],
        [rows, weight, part, weight_all, other_table, other_rows],
    )
    return density, jnp.transpose(accel, (1, 0, 2))


def solution(mesh):
    groups, members = mesh.devices.shape
    cores = 2 if members % 2 == 0 else 1
    split = Mesh(mesh.devices.reshape(groups, members // cores, cores), ("grp", "z", "core"))
    cells = ("grp", "z", "core")
    return jax.shard_map(
        on_device,
        mesh=split,
        in_specs=(P(cells, None, None), P(cells, None), P(cells, None), P(cells)),
        out_specs=(P(cells, None), P(cells, None, None)),
        check_vma=False,
    )
```

```python
import functools
import math

import jax
import jax.numpy as jnp
from jax import lax
from jax.experimental import pallas as pl
from jax.experimental.pallas import tpu as pltpu
from jax.sharding import Mesh
from jax.sharding import PartitionSpec as P


NORM = 21.0 / (16.0 * math.pi)
TINY = 1e-30
ROWS = 8
BATCH = 16
CHUNK = 16
VMEM_LIMIT = 24 * 1024 * 1024


def split3(v):
    hi = v.astype(jnp.bfloat16).astype(jnp.float32)
    rest = v - hi
    mid = rest.astype(jnp.bfloat16).astype(jnp.float32)
    return hi, mid, rest - mid


def right_parts(v):
    hi, mid, low = split3(v)
    return jnp.concatenate([hi, mid, hi, low, hi, mid], axis=0)


def left_parts(v):
    hi, mid, low = split3(v)
    return jnp.concatenate([hi, hi, mid, hi, low, mid], axis=0)


def sum_parts(v):
    hi, mid, low = split3(v)
    return jnp.concatenate([hi, mid, low, jnp.zeros_like(low)], axis=0).astype(jnp.bfloat16)


def left_rows(v):
    row = lax.broadcasted_iota(jnp.int32, v.shape, 0)
    return jnp.where(row < 3, -2.0 * v, jnp.where(row == 3, v[4:5], jnp.where(row == 4, 1.0, 0.0)))


def right_rows(v, shift):
    row = lax.broadcasted_iota(jnp.int32, v.shape, 0)
    rows = jnp.where(row < 5, v, 0.0)
    if shift:
        rows = rows + jnp.where(
            row == 0, shift, jnp.where(row == 4, shift * (2.0 * v[0:1] + shift), 0.0)
        )
    return rows


def table_cells(refs, sizes, fn):
    _, depth, cores, own = sizes
    per_ref = depth * own
    for at, ref in enumerate(refs):
        shift = float(at // cores - 1)

        def step(i, carry, ref=ref, at=at, shift=shift):
            fn(at * per_ref + i, ref[i], shift)
            return carry

        lax.fori_loop(0, per_ref, step, 0, unroll=4)


def list_batches(own, counts, cell_of, slot_of):
    made = jnp.int32(0)
    for cell in range(own):

        def step(k, made, cell=cell):
            cell_of[made] = cell
            slot_of[made] = k * BATCH
            return made + 1

        made = lax.fori_loop(0, lax.div(counts[cell], BATCH), step, made)
    return made


def rows_kernel(particles, rows):
    x, y, z, mass, smooth = (particles[k] for k in range(5))
    x, y, z = x - 0.5, y - 0.5, z - 0.5
    made = (x, y, z, jnp.ones_like(x), x * x + y * y + z * z, mass, 1.0 / smooth, jnp.exp(jnp.log(mass) * 0.2))
    for cell in range(particles.shape[1]):
        rows[cell] = jnp.concatenate([m[cell : cell + 1] for m in made], axis=0)


def density_kernel(sizes, index, counts, own_ref, entropy, *rest):
    refs, (density, weight, table, nu_rows, left, total, ahead, cell_of, slot_of) = (
        rest[:-9],
        rest[-9:],
    )
    own = sizes[3]
    width = own_ref.shape[2]

    def fill(at, v, shift):
        nu = v[7:8]
        table[at] = right_parts((nu * nu) * right_rows(v, shift)).astype(jnp.bfloat16)
        nu_rows[at] = jnp.concatenate(
            [jnp.broadcast_to(4.0 * nu, v.shape), jnp.broadcast_to(5.0 * nu, v.shape)], axis=0
        )

    table_cells(refs, sizes, fill)
    for cell in range(own):
        v = own_ref[cell]
        parts = left_parts((4.0 * (v[6:7] * v[6:7])) * left_rows(v))
        left[cell] = jnp.transpose(parts).astype(jnp.bfloat16)
    total[...] = jnp.zeros_like(total)
    batches = list_batches(own, counts, cell_of, slot_of)

    def slots(batch, pair):
        cell, slot = cell_of[batch], slot_of[batch] + 2 * pair
        return index[cell, slot], index[cell, slot + 1]

    pairs = BATCH // 2

    def fill_pair(batch, half, pair):
        first, second = slots(batch, pair)
        right = jnp.concatenate([table[first], table[second]], axis=1)
        ahead[half, pair] = jnp.dot(
            left[cell_of[batch]], right, preferred_element_type=jnp.float32
        )

    def fill(batch, half):
        for pair in range(pairs):
            fill_pair(batch, half, pair)

    def add(batch, half, later=None):
        sums = [None] * (width // CHUNK)
        if later is not None:
            fill(later, 1 - half)
        for pair in range(pairs):
            first, second = slots(batch, pair)
            nu = jnp.concatenate([nu_rows[first], nu_rows[second]], axis=1)
            nu4 = jnp.concatenate([nu[:ROWS]] * (CHUNK // ROWS), axis=0)
            nu5 = jnp.concatenate([nu[ROWS:]] * (CHUNK // ROWS), axis=0)
            for r in range(width // CHUNK):
                sq = jnp.maximum(ahead[half, pair, r * CHUNK : (r + 1) * CHUNK], TINY)
                base = jnp.maximum(nu4 - sq * lax.rsqrt(sq), 0.0)
                base2 = base * base
                term = (base2 * base2) * (nu5 - base)
                term = term[:, :width] + term[:, width:]
                sums[r] = term if sums[r] is None else sums[r] + term
        cell = cell_of[batch]
        for r in range(width // CHUNK):
            total[cell, r * CHUNK : (r + 1) * CHUNK] += sums[r]

    last = batches - 1
    fill(0, 0)

    def step(k, carry):
        add(2 * k, 0, 2 * k + 1)
        add(2 * k + 1, 1, jnp.minimum(2 * k + 2, last))
        return carry

    lax.fori_loop(0, lax.div(batches, 2), step, 0)

    @pl.when(lax.rem(batches, 2) == 1)
    def _():
        add(last, 0)

    inv = jnp.concatenate([own_ref[cell][6:7] for cell in range(own)], axis=0)
    summed = jnp.concatenate(
        [jnp.sum(jnp.transpose(total[cell]), axis=0, keepdims=True) for cell in range(own)], axis=0
    )
    dens = (NORM / 256.0) * (inv * inv * inv) * summed
    density[...] = dens
    value = entropy[...] * jnp.exp(jnp.log(dens) * (-1.0 / 3.0))
    for copy in range(weight.shape[0]):
        weight[copy] = value


def pair_sums(sizes, index, counts, left, table, rows, total, ahead, cell_of, slot_of):
    own = sizes[3]
    width = table.shape[2]
    pairs = BATCH // 2
    total[...] = jnp.zeros_like(total)
    batches = list_batches(own, counts, cell_of, slot_of)

    def slots(batch, pair):
        cell, slot = cell_of[batch], slot_of[batch] + 2 * pair
        return index[cell, slot], index[cell, slot + 1]

    def fill(batch, half):
        others = []
        for pair in range(pairs):
            first, second = slots(batch, pair)
            others.append(jnp.transpose(jnp.concatenate([table[first], table[second]], axis=0)))
        ahead[half] = jnp.dot(
            jnp.concatenate(others, axis=0),
            left[cell_of[batch]],
            preferred_element_type=jnp.float32,
        )

    def add(batch, half, later=None):
        added = None
        if later is not None:
            fill(later, 1 - half)
        for pair in range(pairs):
            highs, lows = [], []
            for r in range(pair * width, (pair + 1) * width, CHUNK):
                sq = jnp.maximum(ahead[half, r : r + CHUNK], TINY)
                base = jnp.maximum(1.0 - sq * lax.rsqrt(sq), 0.0)
                cube = base * base * base
                high = cube.astype(jnp.bfloat16)
                highs.append(high)
                lows.append((cube - high.astype(jnp.float32)).astype(jnp.bfloat16))
            high = jnp.concatenate(highs, axis=0)
            low = jnp.concatenate(lows, axis=0)
            cubes = jnp.concatenate(
                [
                    jnp.concatenate([high[:, :width], high[:, width:]], axis=0),
                    jnp.concatenate([low[:, :width], low[:, width:]], axis=0),
                ],
                axis=1,
            )
            first, second = slots(batch, pair)
            both = jnp.concatenate([rows[first], rows[second]], axis=1)
            part = jnp.dot(both, cubes, preferred_element_type=jnp.float32)
            added = part if added is None else added + part
        total[cell_of[batch]] += added

    last = batches - 1
    fill(0, 0)

    def step(k, carry):
        add(2 * k, 0, 2 * k + 1)
        add(2 * k + 1, 1, jnp.minimum(2 * k + 2, last))
        return carry

    lax.fori_loop(0, lax.div(batches, 2), step, 0)

    @pl.when(lax.rem(batches, 2) == 1)
    def _():
        add(last, 0)


def folded(total, width):
    both = total[:, :width] + total[:, width:]
    return both[:ROWS] + both[ROWS : 2 * ROWS] + both[2 * ROWS : 3 * ROWS]


def padded_parts(parts):
    pad = jnp.zeros((8 * ROWS - parts.shape[0], parts.shape[1]), parts.dtype)
    return jnp.concatenate([parts, pad], axis=0).astype(jnp.bfloat16)


def block_diagonal(parts):
    pad = jnp.zeros((8 * ROWS - parts.shape[0], parts.shape[1]), parts.dtype)
    whole = jnp.concatenate([parts, pad], axis=0)
    empty = jnp.zeros_like(whole)
    return jnp.concatenate(
        [
            jnp.concatenate([whole, empty], axis=1),
            jnp.concatenate([empty, whole], axis=1),
        ],
        axis=0,
    ).astype(jnp.bfloat16)


def own_kernel(sizes, index, counts, own_ref, *rest):
    refs, (out, other_table, other_rows, left, table, rows, total, ahead, cell_of, slot_of) = (
        rest[:-10],
        rest[-10:],
    )

    def fill(at, v, shift):
        placed = right_rows(v, shift)
        inv2 = v[6:7] * v[6:7]
        table[at] = padded_parts(right_parts(placed))
        rows[at] = sum_parts(v[5:6] * placed)
        other_table[at] = padded_parts(right_parts((0.25 * inv2) * placed))
        other_rows[at] = (v[5:6] * (inv2 * inv2 * v[6:7])) * placed

    table_cells(refs, sizes, fill)
    for cell in range(sizes[3]):
        v = own_ref[cell]
        left[cell] = block_diagonal(left_parts((0.25 * (v[6:7] * v[6:7])) * left_rows(v)))
    pair_sums(sizes, index, counts, left, table, rows, total, ahead, cell_of, slot_of)
    for cell in range(sizes[3]):
        out[cell] = folded(total[cell], own_ref.shape[2])


def other_kernel(
    sizes,
    index,
    counts,
    place,
    own_ref,
    weight_own,
    part,
    weight_all,
    table,
    other_rows,
    out,
    left,
    rows,
    total,
    ahead,
    cell_of,
    slot_of,
):
    groups, depth, cores, own = sizes
    for block in range(3 * cores):
        side, core = block // cores, block % cores
        group = lax.rem(place[0] + side - 1 + groups, groups)

        def fill(step, carry, block=block, core=core, group=group):
            z = lax.rem(place[1] + step, depth)
            source = (group * depth + z) * cores + lax.rem(place[2] + core, cores)
            for cell in range(own):
                at = (block * depth + step) * own + cell
                rows[at] = sum_parts(weight_all[source, cell : cell + 1] * other_rows[at])
            return carry

        lax.fori_loop(0, depth, fill, 0, unroll=2)
    for cell in range(own):
        left[cell] = block_diagonal(left_parts(left_rows(own_ref[cell])))
    pair_sums(sizes, index, counts, left, table, rows, total, ahead, cell_of, slot_of)
    for cell in range(own):
        v = own_ref[cell]
        inv2 = v[6:7] * v[6:7]
        scale = weight_own[0, cell : cell + 1] * (inv2 * inv2 * v[6:7])
        both = scale * part[cell] + folded(total[cell], own_ref.shape[2])
        for k in range(3):
            out[k, cell : cell + 1, :] = (5.0 * NORM) * (
                v[k : k + 1] * both[3:4] - both[k : k + 1]
            )


def call(kernel, out_shape, scratch, scalars, arrays):
    smem = pl.BlockSpec(memory_space=pltpu.SMEM)
    vmem = pl.BlockSpec(memory_space=pltpu.VMEM)
    many = isinstance(out_shape, tuple)
    return pl.pallas_call(
        kernel,
        out_shape=out_shape,
        in_specs=[smem] * len(scalars) + [vmem] * len(arrays),
        out_specs=(vmem,) * len(out_shape) if many else vmem,
        scratch_shapes=scratch,
        compiler_params=pltpu.CompilerParams(vmem_limit_bytes=VMEM_LIMIT),
        cost_estimate=pl.CostEstimate(
            flops=4_000_000_000, bytes_accessed=4_000_000, transcendentals=4_000_000
        ),
    )(*scalars, *arrays)


def on_device(particles, entropy, lists, counts):
    own, _, width = particles.shape
    groups, depth, cores = (lax.axis_size(a) for a in ("grp", "z", "core"))
    sizes = (groups, depth, cores, own)
    place = jnp.stack([lax.axis_index(a) for a in ("grp", "z", "core")]).astype(jnp.int32)

    rows = call(
        rows_kernel,
        jax.ShapeDtypeStruct((own, ROWS, width), jnp.float32),
        [],
        [],
        [jnp.transpose(particles, (1, 0, 2))],
    )

    def shifted(block, axis, by):
        count = lax.axis_size(axis)
        return lax.ppermute(block, axis, [(i, (i - by) % count) for i in range(count)])

    got = {0: rows}
    for by in range(1, depth):
        got[by] = shifted(rows, "z", by)
    column = jnp.concatenate([got[by] for by in range(depth)], axis=0)
    sides = [shifted(column, "grp", -1), column, shifted(column, "grp", 1)]
    refs = []
    for side in sides:
        refs.append(side)
        for by in range(1, cores):
            refs.append(shifted(side, "core", by))

    def table_index(cell_id):
        side = (cell_id // (depth * cores * own) - lax.axis_index("grp") + 1 + groups) % groups
        member = cell_id // own
        z = (member // cores - lax.axis_index("z") + depth) % depth
        core = (member - lax.axis_index("core") + cores) % cores
        return ((side * cores + core) * depth + z) * own + cell_id % own

    index = table_index(lists)
    cells = 3 * cores * depth * own
    shape = jax.ShapeDtypeStruct
    f32, bf16 = jnp.float32, jnp.bfloat16
    most = own * (lists.shape[1] // BATCH)
    order = [pltpu.SMEM((most,), jnp.int32), pltpu.SMEM((most,), jnp.int32)]
    ahead = pltpu.VMEM((2, BATCH // 2, width, 2 * width), f32)
    everyone = groups * depth * cores
    density, weight = call(
        functools.partial(density_kernel, sizes),
        (shape((own, width), f32), shape((everyone, own, width), f32)),
        [
            pltpu.VMEM((cells, 6 * ROWS, width), bf16),
            pltpu.VMEM((cells, 2 * ROWS, width), f32),
            pltpu.VMEM((own, width, 6 * ROWS), bf16),
            pltpu.VMEM((own, width, width), f32),
            ahead,
            *order,
        ],
        [index, counts],
        [rows, entropy, *refs],
    )
    weight_all = lax.all_to_all(weight, ("grp", "z", "core"), 0, 0, tiled=True)
    ahead = pltpu.VMEM((2, BATCH // 2 * width, 2 * width), f32)
    left = pltpu.VMEM((own, 16 * ROWS, 2 * width), bf16)
    table = (cells, 8 * ROWS, width)
    sums = pltpu.VMEM((cells, 4 * ROWS, width), bf16)
    total = pltpu.VMEM((own, 4 * ROWS, 2 * width), f32)
    part, other_table, other_rows = call(
        functools.partial(own_kernel, sizes),
        (shape((own, ROWS, width), f32), shape(table, bf16), shape((cells, ROWS, width), f32)),
        [left, pltpu.VMEM(table, bf16), sums, total, ahead, *order],
        [index, counts],
        [rows, *refs],
    )
    accel = call(
        functools.partial(other_kernel, sizes),
        shape((3, own, width), f32),
        [left, sums, total, ahead, *order],
        [index, counts, place],
        [rows, weight, part, weight_all, other_table, other_rows],
    )
    return density, jnp.transpose(accel, (1, 0, 2))


def solution(mesh):
    groups, members = mesh.devices.shape
    cores = 2 if members % 2 == 0 else 1
    split = Mesh(mesh.devices.reshape(groups, members // cores, cores), ("grp", "z", "core"))
    cells = ("grp", "z", "core")
    return jax.shard_map(
        on_device,
        mesh=split,
        in_specs=(P(cells, None, None), P(cells, None), P(cells, None), P(cells)),
        out_specs=(P(cells, None), P(cells, None, None)),
        check_vma=False,
    )
```
